512 devices in a mesh: comp: 128 (over y, z, core), nest: 4 (over x).
Axes of the slice: x: 4, y: 4, z: 16, core: 2. Of those that a mesh axis runs over, the one named last changes fastest.
Arguments:
- spectra: bfloat16 [1152, 65536], P(None, ('nest', 'comp')), may hold values from 0.006 to 8.5, as said below
- kernel: bfloat16 [1152, 1152], replicated, may hold values from -0.1875 to 0.1875
- wind_gain: float32 [1152], replicated, may hold values from 0.02 to 0.3
- damping: float32 [1152], replicated, may hold values from 0.05 to 0.5
- wind_speed: float32 [65536], P(('nest', 'comp')), may hold values from 0.5 to 2
- class_speed: float32 [8, 32], replicated, may hold values from 0.15 to 0.65
- depth_class: int32 [4, 16384], P('nest'), may hold values from 0 to 7
- cell_of_point: int32 [4, 16384], P('nest'), may hold values from 0 to 16383, each once within a row
- sea_mask: int32 [256, 256], P('nest'), may hold values 0 or 1
- bnd_owner: int32 [4, 256], P('nest'), may hold values from 0 to 127
- bnd_slot: int32 [4, 256], P('nest'), may hold values from 0 to 127
Outputs:
- updated: bfloat16 [1152, 65536], P(None, ('nest', 'comp'))
- boundary: bfloat16 [4, 256, 1152], P('nest', 'comp')
The draws below stay inside these ranges and needn't reach their ends.
Inputs may be any that keep to these rules, and one draw needn't show every extreme that they name: `spectra`: every entry is positive. `cell_of_point`: each row names every cell of its strip once.
All inputs are finite; a program needn't handle non-finite values. No bound on the sum of `sea_mask` on one device may be relied on, other than what follows from the above.
Results may differ from the reference program's by a relative error of at most 0.005.
Values may be sent and summed in bfloat16 or wider, within the bound.
A program may use at most 64 MiB of HBM per device.

```python
import math
import jax
import jax.numpy as jnp
import numpy as np
from jax import lax

NDIR = 36
NFREQ = 32
NCOMP = 1152
NCLASS = 8
PDEV = 128
GY = 256
P_REG = 16384
GX = 256
POINTS = 65536
NB = 256
N_COMP = 128
N_NEST = 4


def draw_spectra(key, part):
    key_freq, key_dir, key_point, key_entry = jax.random.split(jax.random.fold_in(key, 17), 4)
    freq_scale = jnp.exp(jax.random.uniform(key_freq, (NFREQ,), jnp.float32, math.log(0.25), math.log(2.5)))
    dir_scale = jnp.exp(jax.random.uniform(key_dir, (NDIR,), jnp.float32, math.log(0.3), math.log(1.5)))
    point_scale = jnp.exp(jax.random.uniform(key_point, (POINTS,), jnp.float32, math.log(0.3), math.log(1.5)))
    entries = jnp.exp(jax.random.uniform(key_entry, (NCOMP, POINTS), jnp.float32, math.log(0.3), math.log(1.5)))
    comp_scale = (freq_scale[:, None] * dir_scale[None, :]).reshape(NCOMP)
    return (comp_scale[:, None] * point_scale[None, :] * entries).astype(jnp.bfloat16)


def place_ends(drawn, rng, smallest, high):
    longest = drawn.shape.index(max(drawn.shape))
    spots = []
    for shift in (0, 1):
        where = [jax.random.randint(jax.random.fold_in(rng, axis), (), 0, length) for axis, length in enumerate(drawn.shape)]
        where[longest] = (where[longest] + shift) % drawn.shape[longest]
        spots.append(tuple(where))
    return drawn.at[spots[0]].set(smallest).at[spots[1]].set(high)


def level_of(key, shape, shards, smallest, largest):
    level = 1.0
    for dim, blocks in shards:
        draws = jax.random.uniform(jax.random.fold_in(jax.random.fold_in(key, 6), dim), (blocks,), jnp.float32, smallest / len(shards), largest / len(shards))
        level = level * jnp.repeat(jnp.exp(draws), shape[dim] // blocks).reshape((-1,) + (1,) * (len(shape) - 1 - dim))
    return level


def cumulative_ranks(number_of, lean):
    weights = [(1 << 20) // math.isqrt(rank ** lean) + 1 for rank in range(1, number_of + 1)]
    width = 1 + sum(weights) // (1 << 30)
    return np.cumsum(np.array([max(1, weight // width) for weight in weights]))


def ranked(key, extent, amount, skew):
    listing = cumulative_ranks(amount, skew)
    pick = jax.random.randint(jax.random.fold_in(key, 1), extent, 0, int(listing[amount - 1]))
    standing = jnp.searchsorted(jnp.asarray(listing, jnp.int32), pick, side="right")
    return jax.random.permutation(jax.random.fold_in(key, 2), amount)[standing].astype(jnp.int32)


def noise(rng, extent, scale, bound, held_as=jnp.bfloat16):
    drawn = scale * jax.random.normal(rng, extent, jnp.float32)
    return jnp.clip(drawn, min=-bound, max=bound).astype(held_as)


def setup_inputs(seed: int = 0) -> dict:
    key_list = jax.random.split(jax.random.key(seed), 12)
    spectra = draw_spectra(jax.random.fold_in(key_list[11], 71), 0)
    kernel = noise(key_list[1], (NCOMP, NCOMP), NCOMP ** -0.5, 0.1875)
    wind_gain = jnp.clip(jnp.exp(jax.random.uniform(key_list[2], (NCOMP,), jnp.float32, math.log(0.02), math.log(0.3))), 0.02, 0.3)
    damping = jnp.clip(jnp.exp(jax.random.uniform(key_list[3], (NCOMP,), jnp.float32, math.log(0.05), math.log(0.5))), 0.05, 0.5)
    wind_speed = jnp.clip(jnp.exp(math.log(2.0) - 1.3862944 * jax.random.uniform(key_list[4], (POINTS,), jnp.float32) ** level_of(key_list[4], (POINTS,), ((0, 512),), -0.2, 0.2)), 0.5, 2.0)
    class_speed = jnp.clip(jax.random.uniform(key_list[5], (NCLASS, NFREQ), jnp.float32, 0.15, 0.65), 0.15, 0.65)
    depth_class = place_ends(jax.random.randint(key_list[6], (N_NEST, P_REG), 0, NCLASS), jax.random.fold_in(key_list[6], 1), 0, NCLASS - 1).astype(jnp.int32)
    cell_of_point = jax.vmap(lambda own: jax.random.permutation(own, P_REG))(jax.random.split(key_list[7], N_NEST)).reshape((N_NEST, P_REG)).astype(jnp.int32)
    sea_mask = place_ends((jax.random.randint(key_list[8], (GX, GY), 0, 5) < 4).astype(jnp.int32), jax.random.fold_in(key_list[8], 1), 0, 1)
    bnd_owner = place_ends(ranked(key_list[9], (N_NEST, NB), N_COMP, 2), jax.random.fold_in(key_list[9], 3), 0, N_COMP - 1).astype(jnp.int32)
    bnd_slot = place_ends(jax.random.randint(key_list[10], (N_NEST, NB), 0, PDEV), jax.random.fold_in(key_list[10], 1), 0, PDEV - 1).astype(jnp.int32)
    return {"spectra": spectra, "kernel": kernel, "wind_gain": wind_gain, "damping": damping, "wind_speed": wind_speed, "class_speed": class_speed, "depth_class": depth_class, "cell_of_point": cell_of_point, "sea_mask": sea_mask, "bnd_owner": bnd_owner, "bnd_slot": bnd_slot}


def reference(spectra, kernel, wind_gain, damping, wind_speed, class_speed, depth_class, cell_of_point, sea_mask, bnd_owner, bnd_slot):
    offsets = jnp.arange(N_NEST, dtype=jnp.int32) * P_REG
    global_cell = (cell_of_point + offsets[:, None]).reshape(-1).astype(jnp.int32)
    sea_cells = sea_mask.astype(jnp.float32)
    cell_class = jnp.zeros((POINTS,), jnp.int32).at[global_cell].set(depth_class.reshape(-1)).reshape(GX, GY)
    angles = jnp.arange(NDIR, dtype=jnp.int32).astype(jnp.float32) * (2.0 * math.pi / NDIR)
    cosines = jnp.cos(angles)[:, None, None]
    sines = jnp.sin(angles)[:, None, None]

    def one_freq(inputs):
        block, freq_index = inputs
        placed = jnp.zeros((NDIR, POINTS), jnp.bfloat16).at[:, global_cell].set(block)
        energy_field = placed.astype(jnp.float32).reshape(NDIR, GX, GY) * sea_cells
        speed = class_speed[:, freq_index][cell_class][None]
        speed_x = speed * cosines
        speed_y = speed * sines
        plus_x = jnp.maximum(speed_x, 0.0) * energy_field
        minus_x = jnp.minimum(speed_x, 0.0) * energy_field
        plus_y = jnp.maximum(speed_y, 0.0) * energy_field
        minus_y = jnp.minimum(speed_y, 0.0) * energy_field
        zero_row = jnp.zeros((NDIR, 1, GY), jnp.float32)
        zero_column = jnp.zeros((NDIR, GX, 1), jnp.float32)
        inflow_x = jnp.concatenate([zero_row, plus_x[:, :-1]], 1) - jnp.concatenate([minus_x[:, 1:], zero_row], 1)
        inflow_y = jnp.concatenate([zero_column, plus_y[:, :, :-1]], 2) - jnp.concatenate([minus_y[:, :, 1:], zero_column], 2)
        advected = (energy_field - (jnp.abs(speed_x) + jnp.abs(speed_y)) * energy_field + inflow_x + inflow_y) * sea_cells
        return advected.reshape(NDIR, POINTS)[:, global_cell].astype(jnp.bfloat16)

    propagated = lax.map(one_freq, (spectra.reshape(NFREQ, NDIR, POINTS), jnp.arange(NFREQ, dtype=jnp.int32)))
    propagated = propagated.reshape(NCOMP, POINTS)

    point_index = (offsets[:, None] + bnd_owner * PDEV + bnd_slot).reshape(-1).astype(jnp.int32)
    boundary = jnp.take(propagated, point_index, axis=1).T.reshape(N_NEST, NB, NCOMP)

    live_mask = sea_cells.reshape(-1)[global_cell]
    block_size = PDEV * N_NEST
    block_count = POINTS // block_size

    def source_block(inputs):
        block, wind_block, live_block = inputs
        energy = jnp.sum(block, axis=0, dtype=jnp.float32) / NCOMP
        forward = jnp.dot(kernel, block, preferred_element_type=jnp.float32)
        backward = jnp.dot(kernel.T, block, preferred_element_type=jnp.float32)
        cross_terms = (forward * backward).astype(jnp.bfloat16)
        coupling = jnp.dot(kernel, cross_terms, preferred_element_type=jnp.float32)
        growth = 1.0 + wind_gain[:, None] * wind_block[None, :] - damping[:, None] * energy[None, :]
        result = jnp.maximum(block.astype(jnp.float32) * growth + 0.1 * coupling, 0.0) * live_block[None, :]
        return result.astype(jnp.bfloat16)

    blocks = propagated.reshape(NCOMP, block_count, block_size).transpose(1, 0, 2)
    results = lax.map(source_block, (blocks, wind_speed.reshape(block_count, block_size), live_mask.reshape(block_count, block_size)))
    updated = results.transpose(1, 0, 2).reshape(NCOMP, POINTS)
    return updated, boundary
```

```python
import math

import jax
import jax.numpy as jnp
from jax import lax
from jax.sharding import PartitionSpec as P

NDIR = 36


HIGHEST = lax.Precision.HIGHEST


def passed_along(value, axis, steps):
    count = lax.axis_size(axis)
    initial, last = (max(0, -steps), min(count, count - steps))
    return lax.ppermute(value, axis, [(source, source + steps) for source in range(initial, last)])


def body(
    spectra,
    kernel,
    wind_gain,
    damping,
    wind_speed,
    class_speed,
    depth_class,
    cell_of_point,
    sea_mask,
    bnd_owner,
    bnd_slot,
):
    comp_count, slot_count = spectra.shape
    group_size = lax.axis_size("comp")
    my_index = lax.axis_index("comp")
    per_device = comp_count // group_size
    strip_rows, strip_cols = sea_mask.shape
    cell_ids = cell_of_point[0]
    region_size = cell_ids.shape[0]
    sea_cells = sea_mask.astype(jnp.float32)
    fields = lax.all_to_all(spectra, "comp", split_axis=0, concat_axis=1, tiled=True)
    comp_ids = my_index * per_device + jnp.arange(per_device, dtype=jnp.int32)
    freq_ids = comp_ids // NDIR
    dir_ids = comp_ids % NDIR
    angles = dir_ids.astype(jnp.float32) * (2.0 * math.pi / NDIR)
    class_count, freq_count = class_speed.shape
    pick_freq = (freq_ids[:, None] == jnp.arange(freq_count, dtype=jnp.int32)[None, :]).astype(
        jnp.float32
    )
    speed_table = jnp.dot(pick_freq, class_speed.T, precision=HIGHEST)
    cell_class = jnp.zeros((region_size,), jnp.int32).at[cell_ids].set(depth_class[0])
    onehot = (jnp.arange(class_count, dtype=jnp.int32)[:, None] == cell_class[None, :]).astype(
        jnp.float32
    )
    speed = jnp.dot(speed_table, onehot, precision=HIGHEST).reshape(
        per_device, strip_rows, strip_cols
    )
    placed = jnp.zeros((per_device, region_size), jnp.bfloat16).at[:, cell_ids].set(fields)
    energy_field = (
        placed.astype(jnp.float32).reshape(per_device, strip_rows, strip_cols) * sea_cells
    )
    speed_x = speed * jnp.cos(angles)[:, None, None]
    speed_y = speed * jnp.sin(angles)[:, None, None]
    plus_x = jnp.maximum(speed_x, 0.0) * energy_field
    minus_x = jnp.minimum(speed_x, 0.0) * energy_field
    plus_y = jnp.maximum(speed_y, 0.0) * energy_field
    minus_y = jnp.minimum(speed_y, 0.0) * energy_field
    from_prev = passed_along(plus_x[:, -1, :], "nest", 1)
    from_next = passed_along(minus_x[:, 0, :], "nest", -1)
    inflow_x = jnp.concatenate([from_prev[:, None, :], plus_x[:, :-1]], 1) - jnp.concatenate(
        [minus_x[:, 1:], from_next[:, None, :]], 1
    )
    zero_column = jnp.zeros((per_device, strip_rows, 1), jnp.float32)
    inflow_y = jnp.concatenate([zero_column, plus_y[:, :, :-1]], 2) - jnp.concatenate(
        [minus_y[:, :, 1:], zero_column], 2
    )
    advected = (
        energy_field - (jnp.abs(speed_x) + jnp.abs(speed_y)) * energy_field + inflow_x + inflow_y
    ) * sea_cells
    advected_points = jnp.take(advected.reshape(per_device, region_size), cell_ids, axis=1).astype(
        jnp.bfloat16
    )
    owners = bnd_owner[0]
    slot_ids = bnd_slot[0]
    propagated = lax.all_to_all(advected_points, "comp", split_axis=1, concat_axis=0, tiled=True)
    listed_cells = jnp.take(cell_ids, owners * slot_count + slot_ids)
    listed = jnp.take(advected.reshape(per_device, region_size), listed_cells, axis=1).astype(
        jnp.bfloat16
    )
    boundary = lax.all_to_all(listed, "comp", split_axis=1, concat_axis=0, tiled=True).T[None]
    first_point = my_index * slot_count
    my_cells = lax.dynamic_slice_in_dim(cell_ids, first_point, slot_count)
    live_mask = jnp.take(sea_cells.reshape(-1), my_cells)
    energy = jnp.sum(propagated, axis=0, dtype=jnp.float32) / comp_count
    forward = jnp.dot(kernel, propagated, preferred_element_type=jnp.float32)
    backward = lax.dot_general(
        kernel, propagated, (((0,), (0,)), ((), ())), preferred_element_type=jnp.float32
    )
    cross_terms = (forward * backward).astype(jnp.bfloat16)
    coupling = jnp.dot(kernel, cross_terms, preferred_element_type=jnp.float32)
    growth = 1.0 + wind_gain[:, None] * wind_speed[None, :] - damping[:, None] * energy[None, :]
    updated = (
        jnp.maximum(propagated.astype(jnp.float32) * growth + 0.1 * coupling, 0.0)
        * live_mask[None, :]
    ).astype(jnp.bfloat16)
    return (updated, boundary)


def solution(mesh):
    placed = (
        P(None, ("nest", "comp")),
        P(),
        P(),
        P(),
        P(("nest", "comp")),
        P(),
        P("nest", None),
        P("nest", None),
        P("nest", None),
        P("nest", None),
        P("nest", None),
    )
    return jax.shard_map(
        body,
        mesh=mesh,
        in_specs=placed,
        out_specs=(P(None, ("nest", "comp")), P("nest", "comp", None)),
        check_vma=False,
    )
```

```python
import functools
import math

import jax
import jax.numpy as jnp
import numpy as np
from jax import lax
from jax.experimental import pallas as pl
from jax.experimental.pallas import tpu as pltpu
from jax.sharding import PartitionSpec as P

NDIR = 36
NESTED = 2
YDIM, ZDIM = 4, 16
F32, BF16, I32 = jnp.float32, jnp.bfloat16, jnp.int32


def nt(a, b):
    return lax.dot_general(a, b, (((1,), (1,)), ((), ())), preferred_element_type=F32)


def nn(a, b):
    return jnp.dot(a, b, preferred_element_type=F32)


def iota(shape, dim):
    return lax.broadcasted_iota(I32, shape, dim)


def onehot(mask):
    return jnp.where(mask, 1.0, 0.0).astype(BF16)


def step_kernel(
    sizes,
    spec_ref,
    kern_hbm,
    gain_ref,
    damp_ref,
    wind_ref,
    table_ref,
    cos_ref,
    sin_ref,
    class_ref,
    cell_ref,
    sea_ref,
    owner_ref,
    slot_ref,
    upd_ref,
    bnd_ref,
    lo_ref,
    hi_ref,
    cls_ref,
    col_ref,
    row_ref,
    colb_ref,
    rowb_ref,
    lhs_ref,
    acc_ref,
    adv_ref,
    advb_ref,
    last_s,
    main_r1,
    last_r1,
    main_s2,
    pair_s2,
    main_r2,
    pair_r2,
    bpt_ref,
    lastp_ref,
    listp_ref,
    halo_s,
    halo_r,
    prop_ref,
    kern_ref,
    kernt_ref,
    grow_ref,
    damp_b,
    cross_ref,
    kern_sem,
    s1_sem,
    r1_sem,
    s2_sem,
    r2_sem,
    halo_sem,
):
    nc, ncomp, pdev, srows, gy, nclass, nnest = sizes
    yd, zd = YDIM, ZDIM
    whole = 8 * nc
    span = yd * 2 * pdev
    me = lax.axis_index("comp")
    strip = lax.axis_index("nest")
    my_core = lax.rem(me, 2)
    my_z = lax.rem(me // 2, zd)
    my_y = me // (2 * zd)
    nxt = lax.rem(strip + 1, nnest)
    prv = lax.rem(strip + nnest - 1, nnest)

    def offset(j):
        odd = lax.rem(j, 2)
        return zd // 2 + odd * ((j + 1) // 2) - (1 - odd) * (j // 2)

    def chip_of(j, dy):
        return lax.rem(my_y - dy + yd, yd) * zd + lax.rem(my_z - offset(j) + 2 * zd, zd)

    def chip_to(j, dy):
        return lax.rem(my_y + dy, yd) * zd + lax.rem(my_z + offset(j), zd)

    def mirror(j):
        odd = lax.rem(j, 2)
        return j + odd * (1 - j // (zd - 1)) - (1 - odd) * ((j + zd - 1) // zd)

    kern_copy = pltpu.make_async_copy(kern_hbm, kern_ref, kern_sem)
    kern_copy.start()

    barrier = pltpu.get_barrier_semaphore()

    def greet(i, _):
        peer = lax.rem(me + i, nc)
        pl.semaphore_signal(barrier, inc=1, device_id={"comp": peer}, device_id_type=pl.DeviceIdType.MESH)
        return 0

    lax.fori_loop(1, nc, greet, 0)
    pl.semaphore_signal(barrier, inc=1, device_id={"nest": nxt}, device_id_type=pl.DeviceIdType.MESH)
    pl.semaphore_signal(barrier, inc=1, device_id={"nest": prv}, device_id_type=pl.DeviceIdType.MESH)

    tail = spec_ref[nc:, :, :].astype(F32).reshape(ncomp - whole, pdev)
    last_s[...] = tail.reshape(ncomp - whole, 1, pdev)
    cells = cell_ref[...]
    lo_ref[...] = jnp.bitwise_and(cells, gy - 1).astype(F32)
    hi_ref[...] = lax.shift_right_logical(cells, int(math.log2(gy))).astype(F32)
    cls_ref[...] = class_ref[...].astype(F32)

    def build(j, _):
        for dy in range(yd):
            for c in range(2):
                src = 2 * chip_of(j, dy) + c
                cols = pl.ds((2 * dy + c) * pdev, pdev)
                lo = lo_ref[pl.ds(src, 1), :]
                hi = hi_ref[pl.ds(src, 1), :]
                col_ref[j, :, cols] = onehot(iota((gy, pdev), 0).astype(F32) == lo)
                row_ref[j, :, cols] = onehot(iota((srows, pdev), 0).astype(F32) == hi)
        return 0

    lax.fori_loop(0, zd, build, 0)

    pl.semaphore_wait(barrier, nc - 1 + 2)

    def first(dest, j):
        pltpu.make_async_remote_copy(
            src_ref=spec_ref.at[dest],
            dst_ref=main_r1.at[me],
            send_sem=s1_sem.at[0],
            recv_sem=r1_sem.at[0, j],
            device_id={"comp": dest},
            device_id_type=pl.DeviceIdType.MESH,
        ).start()
        pltpu.make_async_remote_copy(
            src_ref=last_s.at[dest],
            dst_ref=last_r1.at[me],
            send_sem=s1_sem.at[1],
            recv_sem=r1_sem.at[1, j],
            device_id={"comp": dest},
            device_id_type=pl.DeviceIdType.MESH,
        ).start()

    def send_group(j, _):
        for dy in range(yd):
            for c in range(2):
                first(2 * chip_to(j, dy) + c, j)
        return 0

    lax.fori_loop(0, zd - 1, send_group, 0)
    for dy in range(1, yd):
        for c in range(2):
            first(2 * chip_to(zd - 1, dy) + c, zd - 1)
    first(me + 1 - 2 * my_core, zd - 1)
    main_r1[me] = spec_ref[me]
    last_r1[me] = last_s[me]

    owner_hot = onehot(iota((nc, NESTED * nc), 0) == owner_ref[...])
    slot_hot = iota((pdev, NESTED * nc), 0) == slot_ref[...]

    def listed(ref):
        by_slot = lax.dot_general(
            ref[...].astype(BF16), owner_hot, (((0,), (0,)), ((), ())), preferred_element_type=F32
        )
        return jnp.sum(jnp.where(slot_hot, by_slot, 0.0), axis=0, keepdims=True)

    colb_ref[...] = onehot(iota((gy, NESTED * nc), 0).astype(F32) == listed(lo_ref))
    rowb_ref[...] = onehot(iota((srows, NESTED * nc), 0).astype(F32) == listed(hi_ref))

    kern_copy.wait()
    blocks = ncomp // pdev

    def turn(i, _):
        for k in range(blocks):
            tile = kern_ref[pl.ds(pl.multiple_of(i * pdev, pdev), pdev), k * pdev : (k + 1) * pdev]
            kernt_ref[k * pdev : (k + 1) * pdev, pl.ds(pl.multiple_of(i * pdev, pdev), pdev)] = (
                tile.astype(F32).T.astype(BF16)
            )
        return 0

    lax.fori_loop(0, blocks, turn, 0)

    def factors(i, _):
        rows = pl.ds(pl.multiple_of(i * pdev, pdev), pdev)
        gain = jnp.broadcast_to(gain_ref[pl.ds(i, 1), :], (pdev, pdev)).T
        grow_ref[rows, :] = 1.0 + gain * wind_ref[...]
        damp_b[rows, :] = jnp.broadcast_to(damp_ref[pl.ds(i, 1), :], (pdev, pdev)).T
        return 0

    lax.fori_loop(0, blocks, factors, 0)

    acc_ref[...] = jnp.zeros_like(acc_ref)

    def place(j):
        for dy in range(yd):
            for c in range(2):
                src = 2 * chip_of(j, dy) + c
                cols = pl.ds((2 * dy + c) * pdev, pdev)
                rows = row_ref[j, :, cols].astype(F32)
                values = main_r1[src].astype(F32)
                for k in range(8):
                    lhs_ref[k * srows : (k + 1) * srows, cols] = (values[k : k + 1, :] * rows).astype(BF16)
                lhs_ref[8 * srows : 9 * srows, cols] = (last_r1[src] * rows).astype(BF16)
                lhs_ref[9 * srows :, cols] = (cls_ref[pl.ds(src, 1), :] * rows).astype(BF16)
        acc_ref[...] += nt(lhs_ref[...], col_ref[j])

    def arrived(sem, ref, count):
        pltpu.make_async_copy(ref.at[pl.ds(0, count)], ref.at[pl.ds(0, count)], sem).wait()

    def take(j, _):
        arrived(r1_sem.at[0, j], main_r1, 2 * yd)
        arrived(r1_sem.at[1, j], last_r1, 2 * yd)
        place(j)
        return 0

    lax.fori_loop(0, zd - 1, take, 0)
    arrived(r1_sem.at[0, zd - 1], main_r1, 2 * yd - 1)
    arrived(r1_sem.at[1, zd - 1], last_r1, 2 * yd - 1)
    place(zd - 1)

    sea = sea_ref[...].astype(F32)
    cell_class = acc_ref[9 * srows :, :]

    def comp_of(c):
        return 8 * me + c if c < 8 else whole + me

    def fluxes(c, top, count):
        comp = comp_of(c)
        freq = comp // NDIR
        energy = acc_ref[c * srows + top : c * srows + top + count, :] * sea[top : top + count]
        here = cell_class[top : top + count]
        speed = jnp.zeros_like(energy)
        for q in range(nclass):
            speed = jnp.where(here == float(q), table_ref[q, freq], speed)
        sx = speed * cos_ref[comp]
        sy = speed * sin_ref[comp]
        return energy, sx, sy

    edge = min(8, srows)
    for c in range(9):
        energy, sx, _ = fluxes(c, srows - edge, edge)
        halo_s[0, c : c + 1, :] = (jnp.maximum(sx, 0.0) * energy)[edge - 1 :, :]
        energy, sx, _ = fluxes(c, 0, edge)
        halo_s[1, c : c + 1, :] = (jnp.minimum(sx, 0.0) * energy)[:1, :]
    halo = [
        pltpu.make_async_remote_copy(
            src_ref=halo_s.at[k],
            dst_ref=halo_r.at[k],
            send_sem=halo_sem.at[0, k],
            recv_sem=halo_sem.at[1, k],
            device_id={"nest": peer},
            device_id_type=pl.DeviceIdType.MESH,
        )
        for k, peer in enumerate((nxt, prv))
    ]
    for copy in halo:
        copy.start()
    row_id = iota((srows, gy), 0)
    col_id = iota((srows, gy), 1)
    for c in range(9):
        energy, sx, sy = fluxes(c, 0, srows)
        plus_x = jnp.maximum(sx, 0.0) * energy
        minus_x = jnp.minimum(sx, 0.0) * energy
        plus_y = jnp.maximum(sy, 0.0) * energy
        minus_y = jnp.minimum(sy, 0.0) * energy
        inflow_x = jnp.where(row_id > 0, pltpu.roll(plus_x, 1, 0), 0.0) - jnp.where(
            row_id < srows - 1, pltpu.roll(minus_x, srows - 1, 0), 0.0
        )
        inflow_y = jnp.where(col_id > 0, pltpu.roll(plus_y, 1, 1), 0.0) - jnp.where(
            col_id < gy - 1, pltpu.roll(minus_y, gy - 1, 1), 0.0
        )
        adv_ref[c] = energy - (jnp.abs(sx) + jnp.abs(sy)) * energy + inflow_x + inflow_y
    for copy in halo:
        copy.wait()
    for c in range(9):
        from_prev = jnp.where(strip > 0, halo_r[0, c : c + 1, :], 0.0)
        from_next = jnp.where(strip < nnest - 1, halo_r[1, c : c + 1, :], 0.0)
        edges = jnp.where(row_id == 0, from_prev, 0.0) - jnp.where(row_id == srows - 1, from_next, 0.0)
        advb_ref[c * srows : (c + 1) * srows, :] = ((adv_ref[c] + edges) * sea).astype(BF16)

    def pick(cols, rows, count):
        found = nn(advb_ref[...], cols).reshape(9, srows, count)
        return jnp.sum(found * rows.astype(F32)[None], axis=1)

    at_list = pick(colb_ref[...], rowb_ref[...], NESTED * nc)
    padded = jnp.concatenate([at_list, jnp.zeros((7, NESTED * nc), F32)], axis=0)
    padded = jnp.concatenate([padded, padded, jnp.zeros((pdev - 32, NESTED * nc), F32)], axis=0).astype(BF16)
    half = [
        nt(onehot(iota((nc, NESTED * nc), 1) == NESTED * iota((nc, NESTED * nc), 0) + k), padded) for k in range(NESTED)
    ]
    bpt_ref[...] = jnp.where(iota((nc, pdev), 1) < 16, half[0], half[1])

    def second(dest, j):
        pltpu.make_async_remote_copy(
            src_ref=main_s2.at[dest],
            dst_ref=main_r2.at[me],
            send_sem=s2_sem.at[0],
            recv_sem=r2_sem.at[0, j],
            device_id={"comp": dest},
            device_id_type=pl.DeviceIdType.MESH,
        ).start()
        pltpu.make_async_remote_copy(
            src_ref=pair_s2.at[dest],
            dst_ref=pair_r2.at[me],
            send_sem=s2_sem.at[1],
            recv_sem=r2_sem.at[1, j],
            device_id={"comp": dest},
            device_id_type=pl.DeviceIdType.MESH,
        ).start()

    def give(j):
        for dy in range(yd):
            cols = pl.ds(dy * 2 * pdev, 2 * pdev)
            values = pick(col_ref[j, :, cols], row_ref[j, :, cols], 2 * pdev)
            for c in range(2):
                dest = 2 * chip_of(j, dy) + c
                mine = values[:, c * pdev : (c + 1) * pdev]
                main_s2[dest] = mine[:8].astype(BF16)
                pair_s2[dest] = jnp.concatenate([mine[8:], bpt_ref[pl.ds(dest, 1), :]], axis=0).astype(BF16)

    def give_group(j, _):
        give(j)
        for dy in range(yd):
            for c in range(2):
                second(2 * chip_of(j, dy) + c, mirror(j))
        return 0

    lax.fori_loop(0, zd - 1, give_group, 0)
    give(zd - 1)
    for dy in range(1, yd):
        for c in range(2):
            second(2 * chip_of(zd - 1, dy) + c, zd - 1)
    second(me + 1 - 2 * my_core, zd - 1)
    main_r2[me] = main_s2[me]
    pair_r2[me] = pair_s2[me]

    own = pl.ds(pl.multiple_of(my_core * pdev, pdev), pdev)
    at_slots = nn(sea.astype(BF16), col_ref[zd - 1, :, own]) * row_ref[zd - 1, :, own].astype(F32)
    live = jnp.sum(at_slots, axis=0, keepdims=True)

    def collect(j, _):
        arrived(r2_sem.at[0, j], main_r2, 2 * yd)
        arrived(r2_sem.at[1, j], pair_r2, 2 * yd)
        return 0

    lax.fori_loop(0, zd - 1, collect, 0)
    arrived(r2_sem.at[0, zd - 1], main_r2, 2 * yd - 1)
    arrived(r2_sem.at[1, zd - 1], pair_r2, 2 * yd - 1)
    total = jnp.zeros((8, pdev), F32)
    for i in range(nc // 2):
        upper = main_r2[2 * i].astype(F32)
        lower = main_r2[2 * i + 1].astype(F32)
        total = total + upper + lower
        prop_ref[16 * i : 16 * i + 16, :] = jnp.concatenate([upper, lower], axis=0).astype(BF16)
    for i in range(nc):
        pair = pair_r2[i].astype(F32)
        lastp_ref[i : i + 1, :] = pair[:1]
        listp_ref[i : i + 1, :] = pair[1:]
    prop_ref[whole:, :] = lastp_ref[...].astype(BF16)
    energy = (jnp.sum(total, axis=0, keepdims=True) + jnp.sum(lastp_ref[...], axis=0, keepdims=True)) / ncomp

    got = listp_ref[...].astype(BF16)
    wanted = iota((pdev, ncomp), 1)
    owner_row = jnp.where(wanted < whole, wanted // 8, wanted - whole)
    which = jnp.where(wanted < whole, wanted % 8, 8)
    for k in range(NESTED):
        spread = nn(got, onehot(iota((pdev, ncomp), 0) == 16 * k + which))
        keep = iota((nc, ncomp), 0) == owner_row[:nc]
        bnd_ref[k : k + 1, :] = jnp.sum(jnp.where(keep, spread, 0.0), axis=0, keepdims=True).astype(BF16)

    def cross(i, _):
        rows = pl.ds(pl.multiple_of(i * pdev, pdev), pdev)
        forward = nn(kern_ref[rows, :], prop_ref[...])
        backward = nn(kernt_ref[rows, :], prop_ref[...])
        cross_ref[rows, :] = (forward * backward).astype(BF16)
        return 0

    lax.fori_loop(0, blocks, cross, 0)

    def finish(i, _):
        rows = pl.ds(pl.multiple_of(i * pdev, pdev), pdev)
        coupling = nn(kern_ref[rows, :], cross_ref[...])
        growth = grow_ref[rows, :] - damp_b[rows, :] * energy
        value = jnp.maximum(prop_ref[rows, :].astype(F32) * growth + 0.1 * coupling, 0.0) * live
        upd_ref[rows, :] = value.astype(BF16)
        return 0

    lax.fori_loop(0, blocks, finish, 0)

    arrived(s1_sem.at[0], main_r1, nc - 1)
    arrived(s1_sem.at[1], last_r1, nc - 1)
    arrived(s2_sem.at[0], main_r2, nc - 1)
    arrived(s2_sem.at[1], pair_r2, nc - 1)


def body(
    spectra,
    kernel,
    wind_gain,
    damping,
    wind_speed,
    class_speed,
    depth_class,
    cell_of_point,
    sea_mask,
    bnd_owner,
    bnd_slot,
):
    ncomp, pdev = spectra.shape
    nc = lax.axis_size("comp")
    nnest = lax.axis_size("nest")
    srows, gy = sea_mask.shape
    nclass = class_speed.shape[0]
    blocks = ncomp // pdev
    angles = np.arange(NDIR, dtype=np.float32) * np.float32(2.0 * math.pi / NDIR)
    comp_dir = np.arange(ncomp) % NDIR
    cosines = jnp.asarray(np.cos(angles)[comp_dir], F32)
    sines = jnp.asarray(np.sin(angles)[comp_dir], F32)
    vmem, smem = pl.BlockSpec(memory_space=pltpu.VMEM), pl.BlockSpec(memory_space=pltpu.SMEM)
    sizes = (nc, ncomp, pdev, srows, gy, nclass, nnest)
    span = YDIM * 2 * pdev
    updated, boundary = pl.pallas_call(
        functools.partial(step_kernel, sizes),
        out_shape=(
            jax.ShapeDtypeStruct((ncomp, pdev), BF16),
            jax.ShapeDtypeStruct((NESTED, ncomp), BF16),
        ),
        in_specs=[vmem, pl.BlockSpec(memory_space=pl.ANY), vmem, vmem, vmem, smem, smem, smem] + [vmem] * 5,
        out_specs=(vmem, vmem),
        scratch_shapes=[
            pltpu.VMEM((nc, pdev), F32),
            pltpu.VMEM((nc, pdev), F32),
            pltpu.VMEM((nc, pdev), F32),
            pltpu.VMEM((ZDIM, gy, span), BF16),
            pltpu.VMEM((ZDIM, srows, span), BF16),
            pltpu.VMEM((gy, NESTED * nc), BF16),
            pltpu.VMEM((srows, NESTED * nc), BF16),
            pltpu.VMEM((10 * srows, span), BF16),
            pltpu.VMEM((10 * srows, gy), F32),
            pltpu.VMEM((9, srows, gy), F32),
            pltpu.VMEM((9 * srows, gy), BF16),
            pltpu.VMEM((nc, 1, pdev), F32),
            pltpu.VMEM((nc, 8, pdev), BF16),
            pltpu.VMEM((nc, 1, pdev), F32),
            pltpu.VMEM((nc, 8, pdev), BF16),
            pltpu.VMEM((nc, 2, pdev), BF16),
            pltpu.VMEM((nc, 8, pdev), BF16),
            pltpu.VMEM((nc, 2, pdev), BF16),
            pltpu.VMEM((nc, pdev), F32),
            pltpu.VMEM((nc, pdev), F32),
            pltpu.VMEM((nc, pdev), F32),
            pltpu.VMEM((2, 16, gy), F32),
            pltpu.VMEM((2, 16, gy), F32),
            pltpu.VMEM((ncomp, pdev), BF16),
            pltpu.VMEM((ncomp, ncomp), BF16),
            pltpu.VMEM((ncomp, ncomp), BF16),
            pltpu.VMEM((ncomp, pdev), F32),
            pltpu.VMEM((ncomp, pdev), F32),
            pltpu.VMEM((ncomp, pdev), BF16),
            pltpu.SemaphoreType.DMA,
            pltpu.SemaphoreType.DMA((2,)),
            pltpu.SemaphoreType.DMA((2, ZDIM)),
            pltpu.SemaphoreType.DMA((2,)),
            pltpu.SemaphoreType.DMA((2, ZDIM)),
            pltpu.SemaphoreType.DMA((2, 2)),
        ],
        compiler_params=pltpu.CompilerParams(collective_id=0, has_side_effects=True),
    )(
        spectra.reshape(ncomp // 8, 8, pdev),
        kernel,
        wind_gain.reshape(blocks, pdev),
        damping.reshape(blocks, pdev),
        wind_speed.reshape(1, pdev),
        class_speed,
        cosines,
        sines,
        depth_class.reshape(nc, pdev),
        cell_of_point.reshape(nc, pdev),
        sea_mask,
        bnd_owner,
        bnd_slot,
    )
    return updated, boundary[None]


def solution(mesh):
    placed = (
        P(None, ("nest", "comp")),
        P(),
        P(),
        P(),
        P(("nest", "comp")),
        P(),
        P("nest", None),
        P("nest", None),
        P("nest", None),
        P("nest", None),
        P("nest", None),
    )
    return jax.shard_map(
        body,
        mesh=mesh,
        in_specs=placed,
        out_specs=(P(None, ("nest", "comp")), P("nest", "comp", None)),
        check_vma=False,
    )
```

```python
import functools
import math

import jax
import jax.numpy as jnp
import numpy as np
from jax import lax
from jax.experimental import pallas as pl
from jax.experimental.pallas import tpu as pltpu
from jax.sharding import PartitionSpec as P

NDIR = 36
NESTED = 2
YDIM, ZDIM = 4, 16
F32, BF16, I32 = jnp.float32, jnp.bfloat16, jnp.int32


def nt(a, b):
    return lax.dot_general(a, b, (((1,), (1,)), ((), ())), preferred_element_type=F32)


def nn(a, b):
    return jnp.dot(a, b, preferred_element_type=F32)


def iota(shape, dim):
    return lax.broadcasted_iota(I32, shape, dim)


def onehot(mask):
    return jnp.where(mask, 1.0, 0.0).astype(BF16)


def step_kernel(
    sizes,
    kern_hbm,
    spec_hbm,
    gain_hbm,
    damp_hbm,
    wind_hbm,
    table_hbm,
    cos_hbm,
    sin_hbm,
    class_hbm,
    cell_hbm,
    sea_hbm,
    owner_hbm,
    slot_hbm,
    upd_ref,
    bnd_ref,
    spec_ref,
    gain_ref,
    damp_ref,
    wind_ref,
    table_ref,
    cos_ref,
    sin_ref,
    class_ref,
    cell_ref,
    sea_ref,
    owner_ref,
    slot_ref,
    lo_ref,
    hi_ref,
    cls_ref,
    col_ref,
    row_ref,
    colb_ref,
    rowb_ref,
    lhs_ref,
    acc_ref,
    speed_ref,
    adv_ref,
    advb_ref,
    last_s,
    main_r1,
    last_r1,
    main_s2,
    pair_s2,
    main_r2,
    pair_r2,
    bpt_ref,
    lastp_ref,
    listp_ref,
    halo_s,
    halo_r,
    prop_ref,
    kern_ref,
    kernt_ref,
    grow_ref,
    damp_b,
    cross_ref,
    kern_sem,
    load_sem,
    s1_sem,
    r1_sem,
    s2_sem,
    r2_sem,
    halo_sem,
):
    nc, ncomp, pdev, srows, gy, nclass, nnest = sizes
    yd, zd = YDIM, ZDIM
    whole = 8 * nc
    span = yd * 2 * pdev
    me = lax.axis_index("comp")
    strip = lax.axis_index("nest")
    my_core = lax.rem(me, 2)
    my_z = lax.rem(me // 2, zd)
    my_y = me // (2 * zd)
    nxt = lax.rem(strip + 1, nnest)
    prv = lax.rem(strip + nnest - 1, nnest)

    def offset(j):
        i = (j + 1) // 2
        odd = lax.rem(i, 2)
        far = odd * ((i + 1) // 2) + (1 - odd) * (zd // 2 - i // 2)
        return lax.rem(zd + (1 - 2 * lax.rem(j, 2)) * far, zd) * (1 - j // (zd - 1))

    def far_first(t):
        far = zd // 2 - (t + 1) // 2
        outer = far // (zd // 2 - (zd // 2 - 1) // 2)
        i = outer * (zd - 2 * far) + (1 - outer) * (2 * far - 1)
        return (2 * i - lax.rem(t, 2)) * ((t + zd - 1) // zd)

    def chip_of(j, dy):
        return lax.rem(my_y - dy + yd, yd) * zd + lax.rem(my_z - offset(j) + 2 * zd, zd)

    def chip_to(j, dy):
        return lax.rem(my_y + dy, yd) * zd + lax.rem(my_z + offset(j), zd)

    def mirror(j):
        odd = lax.rem(j, 2)
        return j + odd * (1 - j // (zd - 1)) - (1 - odd) * ((j + zd - 1) // zd)

    kern_copy = pltpu.make_async_copy(kern_hbm, kern_ref, kern_sem)
    held = (
        (cell_hbm, cell_ref),
        (spec_hbm, spec_ref),
        (class_hbm, class_ref),
        (gain_hbm, gain_ref),
        (damp_hbm, damp_ref),
        (wind_hbm, wind_ref),
        (table_hbm, table_ref),
        (cos_hbm, cos_ref),
        (sin_hbm, sin_ref),
        (sea_hbm, sea_ref),
        (owner_hbm, owner_ref),
        (slot_hbm, slot_ref),
    )
    loads = [pltpu.make_async_copy(far, near, load_sem.at[k]) for k, (far, near) in enumerate(held)]
    for load in loads:
        load.start()
    kern_copy.start()

    barrier = pltpu.get_barrier_semaphore()

    def greet(peer):
        pl.semaphore_signal(barrier, inc=1, device_id=peer, device_id_type=pl.DeviceIdType.MESH)

    def greet_group(j, _):
        for dy in range(yd):
            for c in range(2):
                greet({"comp": 2 * chip_to(j, dy) + c})
        return 0

    lax.fori_loop(0, zd - 1, greet_group, 0)
    for dy in range(1, yd):
        for c in range(2):
            greet({"comp": 2 * chip_to(zd - 1, dy) + c})
    greet({"comp": me + 1 - 2 * my_core})
    greet({"nest": nxt})
    greet({"nest": prv})

    for load in loads:
        load.wait()

    tail = spec_ref[nc:, :, :].astype(F32).reshape(ncomp - whole, pdev)
    last_s[...] = tail.reshape(ncomp - whole, 1, pdev)
    cells = cell_ref[...]
    lo_ref[...] = jnp.bitwise_and(cells, gy - 1).astype(F32)
    hi_ref[...] = lax.shift_right_logical(cells, int(math.log2(gy))).astype(F32)
    cls_ref[...] = class_ref[...].astype(F32)

    def build(j, _):
        for dy in range(yd):
            for c in range(2):
                src = 2 * chip_of(j, dy) + c
                cols = pl.ds((2 * dy + c) * pdev, pdev)
                lo = lo_ref[pl.ds(src, 1), :]
                hi = hi_ref[pl.ds(src, 1), :]
                col_ref[j, :, cols] = onehot(iota((gy, pdev), 0).astype(F32) == lo)
                row_ref[j, :, cols] = onehot(iota((srows, pdev), 0).astype(F32) == hi)
        return 0

    lax.fori_loop(0, zd, build, 0)

    pl.semaphore_wait(barrier, nc - 1 + 2)

    def first(dest, j):
        pltpu.make_async_remote_copy(
            src_ref=spec_ref.at[dest],
            dst_ref=main_r1.at[me],
            send_sem=s1_sem.at[0],
            recv_sem=r1_sem.at[0, j],
            device_id={"comp": dest},
            device_id_type=pl.DeviceIdType.MESH,
        ).start()
        pltpu.make_async_remote_copy(
            src_ref=last_s.at[dest],
            dst_ref=last_r1.at[me],
            send_sem=s1_sem.at[1],
            recv_sem=r1_sem.at[1, j],
            device_id={"comp": dest},
            device_id_type=pl.DeviceIdType.MESH,
        ).start()

    def send_group(j, _):
        for dy in range(yd):
            for c in range(2):
                first(2 * chip_to(j, dy) + c, j)
        return 0

    for dy in range(1, yd):
        for c in range(2):
            first(2 * chip_to(zd - 1, dy) + c, zd - 1)
    first(me + 1 - 2 * my_core, zd - 1)
    lax.fori_loop(0, zd - 1, send_group, 0)
    main_r1[me] = spec_ref[me]
    last_r1[me] = last_s[me]

    owner_hot = onehot(iota((nc, NESTED * nc), 0) == owner_ref[...])
    slot_hot = iota((pdev, NESTED * nc), 0) == slot_ref[...]

    def listed(ref):
        by_slot = lax.dot_general(
            ref[...].astype(BF16), owner_hot, (((0,), (0,)), ((), ())), preferred_element_type=F32
        )
        return jnp.sum(jnp.where(slot_hot, by_slot, 0.0), axis=0, keepdims=True)

    colb_ref[...] = onehot(iota((gy, NESTED * nc), 0).astype(F32) == listed(lo_ref))
    rowb_ref[...] = onehot(iota((srows, NESTED * nc), 0).astype(F32) == listed(hi_ref))

    def place_class(j, total):
        parts = []
        for dy in range(yd):
            for c in range(2):
                cols = pl.ds((2 * dy + c) * pdev, pdev)
                values = cls_ref[pl.ds(2 * chip_of(j, dy) + c, 1), :]
                parts.append((values * row_ref[j, :, cols].astype(F32)).astype(BF16))
        return total + nt(jnp.concatenate(parts, axis=1), col_ref[j])

    cell_class = lax.fori_loop(0, zd, place_class, jnp.zeros((srows, gy), F32))
    freqs = (8 * me // NDIR, (8 * me + 7) // NDIR, (whole + me) // NDIR)
    for k, freq in enumerate(freqs):
        speed = jnp.zeros((srows, gy), F32)
        for q in range(nclass):
            speed = jnp.where(cell_class == float(q), table_ref[q, freq], speed)
        speed_ref[k] = speed

    acc_ref[...] = jnp.zeros_like(acc_ref)

    def place(j):
        for dy in range(yd):
            for c in range(2):
                src = 2 * chip_of(j, dy) + c
                cols = pl.ds((2 * dy + c) * pdev, pdev)
                rows = row_ref[j, :, cols]
                values = main_r1[src].astype(F32)
                for k in range(9):
                    value = values[k : k + 1, :] if k < 8 else last_r1[src]
                    if srows % 16 == 0:
                        value = jnp.broadcast_to(value, (16, pdev)).astype(BF16)
                        placed = (rows.reshape(srows // 16, 16, pdev) * value[None]).reshape(srows, pdev)
                    else:
                        placed = rows * value.astype(BF16)
                    lhs_ref[k * srows : (k + 1) * srows, cols] = placed
        acc_ref[...] += nt(lhs_ref[...], col_ref[j])

    def arrived(sem, ref, count):
        pltpu.make_async_copy(ref.at[pl.ds(0, count)], ref.at[pl.ds(0, count)], sem).wait()

    arrived(r1_sem.at[0, zd - 1], main_r1, 2 * yd - 1)
    arrived(r1_sem.at[1, zd - 1], last_r1, 2 * yd - 1)
    place(zd - 1)

    def take(t, _):
        j = lax.rem(t + 1, zd - 1)
        arrived(r1_sem.at[0, j], main_r1, 2 * yd)
        arrived(r1_sem.at[1, j], last_r1, 2 * yd)
        place(j)
        return 0

    lax.fori_loop(0, zd - 1, take, 0)

    sea = sea_ref[...].astype(F32)

    def comp_of(c):
        return 8 * me + c if c < 8 else whole + me

    def fluxes(c, top, count):
        comp = comp_of(c)
        which = comp // NDIR - freqs[0] if c < 8 else 2
        energy = acc_ref[c * srows + top : c * srows + top + count, :] * sea[top : top + count]
        speed = speed_ref[which, top : top + count, :]
        sx = speed * cos_ref[comp]
        sy = speed * sin_ref[comp]
        return energy, sx, sy

    edge = min(8, srows)
    for c in range(9):
        energy, sx, _ = fluxes(c, srows - edge, edge)
        halo_s[0, c : c + 1, :] = (jnp.maximum(sx, 0.0) * energy)[edge - 1 :, :]
        energy, sx, _ = fluxes(c, 0, edge)
        halo_s[1, c : c + 1, :] = (jnp.minimum(sx, 0.0) * energy)[:1, :]
    halo = [
        pltpu.make_async_remote_copy(
            src_ref=halo_s.at[k],
            dst_ref=halo_r.at[k],
            send_sem=halo_sem.at[0, k],
            recv_sem=halo_sem.at[1, k],
            device_id={"nest": peer},
            device_id_type=pl.DeviceIdType.MESH,
        )
        for k, peer in enumerate((nxt, prv))
    ]
    for copy in halo:
        copy.start()
    row_id = iota((srows, gy), 0)
    col_id = iota((srows, gy), 1)
    for c in range(9):
        energy, sx, sy = fluxes(c, 0, srows)
        plus_x = jnp.maximum(sx, 0.0) * energy
        minus_x = jnp.minimum(sx, 0.0) * energy
        plus_y = jnp.maximum(sy, 0.0) * energy
        minus_y = jnp.minimum(sy, 0.0) * energy
        inflow_x = jnp.where(row_id > 0, pltpu.roll(plus_x, 1, 0), 0.0) - jnp.where(
            row_id < srows - 1, pltpu.roll(minus_x, srows - 1, 0), 0.0
        )
        inflow_y = jnp.where(col_id > 0, pltpu.roll(plus_y, 1, 1), 0.0) - jnp.where(
            col_id < gy - 1, pltpu.roll(minus_y, gy - 1, 1), 0.0
        )
        adv_ref[c] = energy - (jnp.abs(sx) + jnp.abs(sy)) * energy + inflow_x + inflow_y
    for copy in halo:
        copy.wait()
    for c in range(9):
        from_prev = jnp.where(strip > 0, halo_r[0, c : c + 1, :], 0.0)
        from_next = jnp.where(strip < nnest - 1, halo_r[1, c : c + 1, :], 0.0)
        edges = jnp.where(row_id == 0, from_prev, 0.0) - jnp.where(row_id == srows - 1, from_next, 0.0)
        advb_ref[c * srows : (c + 1) * srows, :] = ((adv_ref[c] + edges) * sea).astype(BF16)

    def pick(cols, rows, count):
        found = nn(advb_ref[...], cols).reshape(9, srows, count)
        return jnp.sum(found * rows.astype(F32)[None], axis=1)

    at_list = pick(colb_ref[...], rowb_ref[...], NESTED * nc)
    padded = jnp.concatenate([at_list, jnp.zeros((7, NESTED * nc), F32)], axis=0)
    padded = jnp.concatenate([padded, padded, jnp.zeros((pdev - 32, NESTED * nc), F32)], axis=0).astype(BF16)
    half = [
        nt(onehot(iota((nc, NESTED * nc), 1) == NESTED * iota((nc, NESTED * nc), 0) + k), padded) for k in range(NESTED)
    ]
    bpt_ref[...] = jnp.where(iota((nc, pdev), 1) < 16, half[0], half[1])

    def second(dest, j):
        pltpu.make_async_remote_copy(
            src_ref=main_s2.at[dest],
            dst_ref=main_r2.at[me],
            send_sem=s2_sem.at[0],
            recv_sem=r2_sem.at[0, j],
            device_id={"comp": dest},
            device_id_type=pl.DeviceIdType.MESH,
        ).start()
        pltpu.make_async_remote_copy(
            src_ref=pair_s2.at[dest],
            dst_ref=pair_r2.at[me],
            send_sem=s2_sem.at[1],
            recv_sem=r2_sem.at[1, j],
            device_id={"comp": dest},
            device_id_type=pl.DeviceIdType.MESH,
        ).start()

    def give(j):
        for dy in range(yd):
            cols = pl.ds(dy * 2 * pdev, 2 * pdev)
            values = pick(col_ref[j, :, cols], row_ref[j, :, cols], 2 * pdev)
            for c in range(2):
                dest = 2 * chip_of(j, dy) + c
                mine = values[:, c * pdev : (c + 1) * pdev]
                main_s2[dest] = mine[:8].astype(BF16)
                pair_s2[dest] = jnp.concatenate([mine[8:], bpt_ref[pl.ds(dest, 1), :]], axis=0).astype(BF16)

    def give_group(t, _):
        j = far_first(t)
        give(j)
        for dy in range(yd):
            for c in range(2):
                second(2 * chip_of(j, dy) + c, mirror(j))
        return 0

    lax.fori_loop(0, zd - 1, give_group, 0)
    give(zd - 1)
    for dy in range(1, yd):
        for c in range(2):
            second(2 * chip_of(zd - 1, dy) + c, zd - 1)
    second(me + 1 - 2 * my_core, zd - 1)
    main_r2[me] = main_s2[me]
    pair_r2[me] = pair_s2[me]

    own = pl.ds(pl.multiple_of(my_core * pdev, pdev), pdev)
    at_slots = nn(sea.astype(BF16), col_ref[zd - 1, :, own]) * row_ref[zd - 1, :, own].astype(F32)
    live = jnp.sum(at_slots, axis=0, keepdims=True)

    kern_copy.wait()
    blocks = ncomp // pdev

    def turn(i, _):
        for k in range(blocks):
            tile = kern_ref[pl.ds(pl.multiple_of(i * pdev, pdev), pdev), k * pdev : (k + 1) * pdev]
            kernt_ref[k * pdev : (k + 1) * pdev, pl.ds(pl.multiple_of(i * pdev, pdev), pdev)] = (
                tile.T
            )
        return 0

    lax.fori_loop(0, blocks, turn, 0)

    def factors(i, _):
        rows = pl.ds(pl.multiple_of(i * pdev, pdev), pdev)
        gain = jnp.broadcast_to(gain_ref[pl.ds(i, 1), :], (pdev, pdev)).T
        grow_ref[rows, :] = 1.0 + gain * wind_ref[...]
        damp_b[rows, :] = jnp.broadcast_to(damp_ref[pl.ds(i, 1), :], (pdev, pdev)).T
        return 0

    lax.fori_loop(0, blocks, factors, 0)

    def gather(j, total):
        for dy in range(yd):
            chip = chip_of(j, dy)
            upper = main_r2[2 * chip].astype(F32)
            lower = main_r2[2 * chip + 1].astype(F32)
            total = total + (upper + lower)
            prop_ref[pl.ds(pl.multiple_of(16 * chip, 16), 16), :] = jnp.concatenate([upper, lower], axis=0).astype(BF16)
            for c in range(2):
                pair = pair_r2[2 * chip + c].astype(F32)
                lastp_ref[pl.ds(2 * chip + c, 1), :] = pair[:1]
                listp_ref[pl.ds(2 * chip + c, 1), :] = pair[1:]
        return total

    def collect(t, total):
        j = far_first(t)
        arrived(r2_sem.at[0, j], main_r2, 2 * yd)
        arrived(r2_sem.at[1, j], pair_r2, 2 * yd)
        return gather(j, total)

    total = lax.fori_loop(0, zd - 1, collect, jnp.zeros((8, pdev), F32))
    arrived(r2_sem.at[0, zd - 1], main_r2, 2 * yd - 1)
    arrived(r2_sem.at[1, zd - 1], pair_r2, 2 * yd - 1)
    total = gather(zd - 1, total)
    prop_ref[whole:, :] = lastp_ref[...].astype(BF16)
    energy = (jnp.sum(total, axis=0, keepdims=True) + jnp.sum(lastp_ref[...], axis=0, keepdims=True)) / ncomp

    got = listp_ref[...].astype(BF16)
    wanted = iota((pdev, ncomp), 1)
    owner_row = jnp.where(wanted < whole, wanted // 8, wanted - whole)
    which = jnp.where(wanted < whole, wanted % 8, 8)
    for k in range(NESTED):
        spread = nn(got, onehot(iota((pdev, ncomp), 0) == 16 * k + which))
        keep = iota((nc, ncomp), 0) == owner_row[:nc]
        bnd_ref[k : k + 1, :] = jnp.sum(jnp.where(keep, spread, 0.0), axis=0, keepdims=True).astype(BF16)

    big = 3 * pdev if blocks % 3 == 0 else pdev

    def cross(i, _):
        rows = pl.ds(pl.multiple_of(i * big, big), big)
        forward = nn(kern_ref[rows, :], prop_ref[...])
        backward = nn(kernt_ref[rows, :], prop_ref[...])
        cross_ref[rows, :] = (forward * backward).astype(BF16)
        return 0

    lax.fori_loop(0, ncomp // big, cross, 0)

    def finish(i, _):
        rows = pl.ds(pl.multiple_of(i * big, big), big)
        coupling = nn(kern_ref[rows, :], cross_ref[...])
        growth = grow_ref[rows, :] - damp_b[rows, :] * energy
        value = jnp.maximum(prop_ref[rows, :].astype(F32) * growth + 0.1 * coupling, 0.0) * live
        upd_ref[rows, :] = value.astype(BF16)
        return 0

    lax.fori_loop(0, ncomp // big, finish, 0)

    arrived(s1_sem.at[0], main_r1, nc - 1)
    arrived(s1_sem.at[1], last_r1, nc - 1)
    arrived(s2_sem.at[0], main_r2, nc - 1)
    arrived(s2_sem.at[1], pair_r2, nc - 1)


def body(
    spectra,
    kernel,
    wind_gain,
    damping,
    wind_speed,
    class_speed,
    depth_class,
    cell_of_point,
    sea_mask,
    bnd_owner,
    bnd_slot,
):
    ncomp, pdev = spectra.shape
    nc = lax.axis_size("comp")
    nnest = lax.axis_size("nest")
    srows, gy = sea_mask.shape
    nclass = class_speed.shape[0]
    blocks = ncomp // pdev
    angles = np.arange(NDIR, dtype=np.float32) * np.float32(2.0 * math.pi / NDIR)
    comp_dir = np.arange(ncomp) % NDIR
    cosines = jnp.asarray(np.cos(angles)[comp_dir], F32)
    sines = jnp.asarray(np.sin(angles)[comp_dir], F32)
    vmem = pl.BlockSpec(memory_space=pltpu.VMEM)
    sizes = (nc, ncomp, pdev, srows, gy, nclass, nnest)
    span = YDIM * 2 * pdev
    updated, boundary = pl.pallas_call(
        functools.partial(step_kernel, sizes),
        out_shape=(
            jax.ShapeDtypeStruct((ncomp, pdev), BF16),
            jax.ShapeDtypeStruct((NESTED, ncomp), BF16),
        ),
        in_specs=[pl.BlockSpec(memory_space=pl.ANY)] * 13,
        out_specs=(vmem, vmem),
        scratch_shapes=[
            pltpu.VMEM((ncomp // 8, 8, pdev), BF16),
            pltpu.VMEM((blocks, pdev), F32),
            pltpu.VMEM((blocks, pdev), F32),
            pltpu.VMEM((1, pdev), F32),
            pltpu.SMEM(class_speed.shape, F32),
            pltpu.SMEM((ncomp,), F32),
            pltpu.SMEM((ncomp,), F32),
            pltpu.VMEM((nc, pdev), I32),
            pltpu.VMEM((nc, pdev), I32),
            pltpu.VMEM((srows, gy), I32),
            pltpu.VMEM((1, NESTED * nc), I32),
            pltpu.VMEM((1, NESTED * nc), I32),
            pltpu.VMEM((nc, pdev), F32),
            pltpu.VMEM((nc, pdev), F32),
            pltpu.VMEM((nc, pdev), F32),
            pltpu.VMEM((ZDIM, gy, span), BF16),
            pltpu.VMEM((ZDIM, srows, span), BF16),
            pltpu.VMEM((gy, NESTED * nc), BF16),
            pltpu.VMEM((srows, NESTED * nc), BF16),
            pltpu.VMEM((9 * srows, span), BF16),
            pltpu.VMEM((9 * srows, gy), F32),
            pltpu.VMEM((3, srows, gy), F32),
            pltpu.VMEM((9, srows, gy), F32),
            pltpu.VMEM((9 * srows, gy), BF16),
            pltpu.VMEM((nc, 1, pdev), F32),
            pltpu.VMEM((nc, 8, pdev), BF16),
            pltpu.VMEM((nc, 1, pdev), F32),
            pltpu.VMEM((nc, 8, pdev), BF16),
            pltpu.VMEM((nc, 2, pdev), BF16),
            pltpu.VMEM((nc, 8, pdev), BF16),
            pltpu.VMEM((nc, 2, pdev), BF16),
            pltpu.VMEM((nc, pdev), F32),
            pltpu.VMEM((nc, pdev), F32),
            pltpu.VMEM((nc, pdev), F32),
            pltpu.VMEM((2, 16, gy), F32),
            pltpu.VMEM((2, 16, gy), F32),
            pltpu.VMEM((ncomp, pdev), BF16),
            pltpu.VMEM((ncomp, ncomp), BF16),
            pltpu.VMEM((ncomp, ncomp), BF16),
            pltpu.VMEM((ncomp, pdev), F32),
            pltpu.VMEM((ncomp, pdev), F32),
            pltpu.VMEM((ncomp, pdev), BF16),
            pltpu.SemaphoreType.DMA,
            pltpu.SemaphoreType.DMA((12,)),
            pltpu.SemaphoreType.DMA((2,)),
            pltpu.SemaphoreType.DMA((2, ZDIM)),
            pltpu.SemaphoreType.DMA((2,)),
            pltpu.SemaphoreType.DMA((2, ZDIM)),
            pltpu.SemaphoreType.DMA((2, 2)),
        ],
        compiler_params=pltpu.CompilerParams(collective_id=0, has_side_effects=True),
    )(
        kernel,
        spectra.reshape(ncomp // 8, 8, pdev),
        wind_gain.reshape(blocks, pdev),
        damping.reshape(blocks, pdev),
        wind_speed.reshape(1, pdev),
        class_speed,
        cosines,
        sines,
        depth_class.reshape(nc, pdev),
        cell_of_point.reshape(nc, pdev),
        sea_mask,
        bnd_owner,
        bnd_slot,
    )
    return updated, boundary[None]


def solution(mesh):
    placed = (
        P(None, ("nest", "comp")),
        P(),
        P(),
        P(),
        P(("nest", "comp")),
        P(),
        P("nest", None),
        P("nest", None),
        P("nest", None),
        P("nest", None),
        P("nest", None),
    )
    return jax.shard_map(
        body,
        mesh=mesh,
        in_specs=placed,
        out_specs=(P(None, ("nest", "comp")), P("nest", "comp", None)),
        check_vma=False,
    )
```

```python
import functools
import math

import jax
import jax.numpy as jnp
import numpy as np
from jax import lax
from jax.experimental import pallas as pl
from jax.experimental.pallas import tpu as pltpu
from jax.sharding import PartitionSpec as P

NDIR = 36
NESTED = 2
YDIM, ZDIM = 4, 16
F32, BF16, I32 = jnp.float32, jnp.bfloat16, jnp.int32


def nt(a, b):
    return lax.dot_general(a, b, (((1,), (1,)), ((), ())), preferred_element_type=F32)


def nn(a, b):
    return jnp.dot(a, b, preferred_element_type=F32)


def iota(shape, dim):
    return lax.broadcasted_iota(I32, shape, dim)


def onehot(mask):
    return jnp.where(mask, 1.0, 0.0).astype(BF16)


def step_kernel(
    sizes,
    kern_hbm,
    spec_hbm,
    gain_hbm,
    damp_hbm,
    wind_hbm,
    table_hbm,
    cos_hbm,
    sin_hbm,
    class_hbm,
    cell_hbm,
    sea_hbm,
    owner_hbm,
    slot_hbm,
    upd_ref,
    bnd_ref,
    spec_ref,
    gain_ref,
    damp_ref,
    wind_ref,
    table_ref,
    cos_ref,
    sin_ref,
    class_ref,
    cell_ref,
    sea_ref,
    owner_ref,
    slot_ref,
    lo_ref,
    hi_ref,
    cls_ref,
    col_ref,
    row_ref,
    colb_ref,
    rowb_ref,
    lhs_ref,
    acc_ref,
    speed_ref,
    adv_ref,
    advb_ref,
    last_s,
    main_r1,
    last_r1,
    main_s2,
    main_r2,
    bpt_ref,
    lastp_ref,
    listp_ref,
    halo_s,
    halo_r,
    prop_ref,
    kern_ref,
    kernt_ref,
    grow_ref,
    damp_b,
    cross_ref,
    kern_sem,
    load_sem,
    s1_sem,
    r1_sem,
    s2_sem,
    r2_sem,
    halo_sem,
):
    nc, ncomp, pdev, srows, gy, nclass, nnest = sizes
    yd, zd = YDIM, ZDIM
    whole = 8 * nc
    span = yd * 2 * pdev
    me = lax.axis_index("comp")
    strip = lax.axis_index("nest")
    my_core = lax.rem(me, 2)
    my_z = lax.rem(me // 2, zd)
    my_y = me // (2 * zd)
    nxt = lax.rem(strip + 1, nnest)
    prv = lax.rem(strip + nnest - 1, nnest)

    def offset(j):
        i = (j + 1) // 2
        odd = lax.rem(i, 2)
        far = odd * ((i + 1) // 2) + (1 - odd) * (zd // 2 - i // 2)
        return lax.rem(zd + (1 - 2 * lax.rem(j, 2)) * far, zd) * (1 - j // (zd - 1))

    def far_first(t):
        far = zd // 2 - (t + 1) // 2
        outer = far // (zd // 2 - (zd // 2 - 1) // 2)
        i = outer * (zd - 2 * far) + (1 - outer) * (2 * far - 1)
        return (2 * i - lax.rem(t, 2)) * ((t + zd - 1) // zd)

    def chip_of(j, dy):
        return lax.rem(my_y - dy + yd, yd) * zd + lax.rem(my_z - offset(j) + 2 * zd, zd)

    def chip_to(j, dy):
        return lax.rem(my_y + dy, yd) * zd + lax.rem(my_z + offset(j), zd)

    def mirror(j):
        odd = lax.rem(j, 2)
        return j + odd * (1 - j // (zd - 1)) - (1 - odd) * ((j + zd - 1) // zd)

    kern_copy = pltpu.make_async_copy(kern_hbm, kern_ref, kern_sem)
    held = (
        (cell_hbm, cell_ref),
        (spec_hbm, spec_ref),
        (class_hbm, class_ref),
        (gain_hbm, gain_ref),
        (damp_hbm, damp_ref),
        (wind_hbm, wind_ref),
        (table_hbm, table_ref),
        (cos_hbm, cos_ref),
        (sin_hbm, sin_ref),
        (sea_hbm, sea_ref),
        (owner_hbm, owner_ref),
        (slot_hbm, slot_ref),
    )
    loads = [pltpu.make_async_copy(far, near, load_sem.at[k]) for k, (far, near) in enumerate(held)]
    for load in loads:
        load.start()
    kern_copy.start()

    barrier = pltpu.get_barrier_semaphore()

    def greet(peer):
        pl.semaphore_signal(barrier, inc=1, device_id=peer, device_id_type=pl.DeviceIdType.MESH)

    def greet_group(j, _):
        for dy in range(yd):
            for c in range(2):
                greet({"comp": 2 * chip_to(j, dy) + c})
        return 0

    lax.fori_loop(0, zd - 1, greet_group, 0)
    for dy in range(1, yd):
        for c in range(2):
            greet({"comp": 2 * chip_to(zd - 1, dy) + c})
    greet({"comp": me + 1 - 2 * my_core})
    greet({"nest": nxt})
    greet({"nest": prv})

    for load in loads:
        load.wait()

    tail = spec_ref[nc:, :, :].astype(F32).reshape(ncomp - whole, pdev)
    last_s[...] = tail.reshape(ncomp - whole, 1, pdev)
    cells = cell_ref[...]
    lo_ref[...] = jnp.bitwise_and(cells, gy - 1).astype(F32)
    hi_ref[...] = lax.shift_right_logical(cells, int(math.log2(gy))).astype(F32)
    cls_ref[...] = class_ref[...].astype(F32)

    def build(j, _):
        for dy in range(yd):
            for c in range(2):
                src = 2 * chip_of(j, dy) + c
                cols = pl.ds((2 * dy + c) * pdev, pdev)
                lo = lo_ref[pl.ds(src, 1), :]
                hi = hi_ref[pl.ds(src, 1), :]
                col_ref[j, :, cols] = onehot(iota((gy, pdev), 0).astype(F32) == lo)
                row_ref[j, :, cols] = onehot(iota((srows, pdev), 0).astype(F32) == hi)
        return 0

    lax.fori_loop(0, zd, build, 0)

    pl.semaphore_wait(barrier, nc - 1 + 2)

    def first(dest, j):
        pltpu.make_async_remote_copy(
            src_ref=spec_ref.at[dest],
            dst_ref=main_r1.at[me],
            send_sem=s1_sem.at[0],
            recv_sem=r1_sem.at[0, j],
            device_id={"comp": dest},
            device_id_type=pl.DeviceIdType.MESH,
        ).start()
        pltpu.make_async_remote_copy(
            src_ref=last_s.at[dest],
            dst_ref=last_r1.at[me],
            send_sem=s1_sem.at[1],
            recv_sem=r1_sem.at[1, j],
            device_id={"comp": dest},
            device_id_type=pl.DeviceIdType.MESH,
        ).start()

    def send_group(j, _):
        for dy in range(yd):
            for c in range(2):
                first(2 * chip_to(j, dy) + c, j)
        return 0

    for dy in range(1, yd):
        for c in range(2):
            first(2 * chip_to(zd - 1, dy) + c, zd - 1)
    first(me + 1 - 2 * my_core, zd - 1)
    lax.fori_loop(0, zd - 1, send_group, 0)
    main_r1[me] = spec_ref[me]
    last_r1[me] = last_s[me]

    owner_hot = onehot(iota((nc, NESTED * nc), 0) == owner_ref[...])
    slot_hot = iota((pdev, NESTED * nc), 0) == slot_ref[...]

    def listed(ref):
        by_slot = lax.dot_general(
            ref[...].astype(BF16), owner_hot, (((0,), (0,)), ((), ())), preferred_element_type=F32
        )
        return jnp.sum(jnp.where(slot_hot, by_slot, 0.0), axis=0, keepdims=True)

    colb_ref[...] = onehot(iota((gy, NESTED * nc), 0).astype(F32) == listed(lo_ref))
    rowb_ref[...] = onehot(iota((srows, NESTED * nc), 0).astype(F32) == listed(hi_ref))

    def place_class(j, total):
        parts = []
        for dy in range(yd):
            for c in range(2):
                cols = pl.ds((2 * dy + c) * pdev, pdev)
                values = cls_ref[pl.ds(2 * chip_of(j, dy) + c, 1), :]
                parts.append((values * row_ref[j, :, cols].astype(F32)).astype(BF16))
        return total + nt(jnp.concatenate(parts, axis=1), col_ref[j])

    cell_class = lax.fori_loop(0, zd, place_class, jnp.zeros((srows, gy), F32))
    freqs = (8 * me // NDIR, (8 * me + 7) // NDIR, (whole + me) // NDIR)
    for k, freq in enumerate(freqs):
        speed = jnp.zeros((srows, gy), F32)
        for q in range(nclass):
            speed = jnp.where(cell_class == float(q), table_ref[q, freq], speed)
        speed_ref[k] = speed

    acc_ref[...] = jnp.zeros_like(acc_ref)

    def place(j):
        for dy in range(yd):
            for c in range(2):
                src = 2 * chip_of(j, dy) + c
                cols = pl.ds((2 * dy + c) * pdev, pdev)
                rows = row_ref[j, :, cols]
                values = main_r1[src].astype(F32)
                for k in range(9):
                    value = values[k : k + 1, :] if k < 8 else last_r1[src]
                    if srows % 16 == 0:
                        value = jnp.broadcast_to(value, (16, pdev)).astype(BF16)
                        placed = (rows.reshape(srows // 16, 16, pdev) * value[None]).reshape(srows, pdev)
                    else:
                        placed = rows * value.astype(BF16)
                    lhs_ref[k * srows : (k + 1) * srows, cols] = placed
        acc_ref[...] += nt(lhs_ref[...], col_ref[j])

    def arrived(sem, ref, count):
        pltpu.make_async_copy(ref.at[pl.ds(0, count)], ref.at[pl.ds(0, count)], sem).wait()

    arrived(r1_sem.at[0, zd - 1], main_r1, 2 * yd - 1)
    arrived(r1_sem.at[1, zd - 1], last_r1, 2 * yd - 1)
    place(zd - 1)

    def take(t, _):
        j = lax.rem(t + 1, zd - 1)
        arrived(r1_sem.at[0, j], main_r1, 2 * yd)
        arrived(r1_sem.at[1, j], last_r1, 2 * yd)
        place(j)
        return 0

    lax.fori_loop(0, zd - 1, take, 0)

    sea = sea_ref[...].astype(F32)

    def comp_of(c):
        return 8 * me + c if c < 8 else whole + me

    def fluxes(c, top, count):
        comp = comp_of(c)
        which = comp // NDIR - freqs[0] if c < 8 else 2
        energy = acc_ref[c * srows + top : c * srows + top + count, :] * sea[top : top + count]
        speed = speed_ref[which, top : top + count, :]
        sx = speed * cos_ref[comp]
        sy = speed * sin_ref[comp]
        return energy, sx, sy

    edge = min(8, srows)
    for c in range(9):
        energy, sx, _ = fluxes(c, srows - edge, edge)
        halo_s[0, c : c + 1, :] = (jnp.maximum(sx, 0.0) * energy)[edge - 1 :, :]
        energy, sx, _ = fluxes(c, 0, edge)
        halo_s[1, c : c + 1, :] = (jnp.minimum(sx, 0.0) * energy)[:1, :]
    halo = [
        pltpu.make_async_remote_copy(
            src_ref=halo_s.at[k],
            dst_ref=halo_r.at[k],
            send_sem=halo_sem.at[0, k],
            recv_sem=halo_sem.at[1, k],
            device_id={"nest": peer},
            device_id_type=pl.DeviceIdType.MESH,
        )
        for k, peer in enumerate((nxt, prv))
    ]
    for copy in halo:
        copy.start()
    row_id = iota((srows, gy), 0)
    col_id = iota((srows, gy), 1)
    for c in range(9):
        energy, sx, sy = fluxes(c, 0, srows)
        plus_x = jnp.maximum(sx, 0.0) * energy
        minus_x = jnp.minimum(sx, 0.0) * energy
        plus_y = jnp.maximum(sy, 0.0) * energy
        minus_y = jnp.minimum(sy, 0.0) * energy
        inflow_x = jnp.where(row_id > 0, pltpu.roll(plus_x, 1, 0), 0.0) - jnp.where(
            row_id < srows - 1, pltpu.roll(minus_x, srows - 1, 0), 0.0
        )
        inflow_y = jnp.where(col_id > 0, pltpu.roll(plus_y, 1, 1), 0.0) - jnp.where(
            col_id < gy - 1, pltpu.roll(minus_y, gy - 1, 1), 0.0
        )
        adv_ref[c] = energy - (jnp.abs(sx) + jnp.abs(sy)) * energy + inflow_x + inflow_y
    for copy in halo:
        copy.wait()
    for c in range(9):
        from_prev = jnp.where(strip > 0, halo_r[0, c : c + 1, :], 0.0)
        from_next = jnp.where(strip < nnest - 1, halo_r[1, c : c + 1, :], 0.0)
        edges = jnp.where(row_id == 0, from_prev, 0.0) - jnp.where(row_id == srows - 1, from_next, 0.0)
        advb_ref[c * srows : (c + 1) * srows, :] = ((adv_ref[c] + edges) * sea).astype(BF16)

    def pick(cols, rows, count):
        found = nn(advb_ref[...], cols).reshape(9, srows, count)
        return jnp.sum(found * rows.astype(F32)[None], axis=1)

    at_list = pick(colb_ref[...], rowb_ref[...], NESTED * nc)
    padded = jnp.concatenate([at_list, jnp.zeros((7, NESTED * nc), F32)], axis=0)
    padded = jnp.concatenate([padded, padded, jnp.zeros((pdev - 32, NESTED * nc), F32)], axis=0).astype(BF16)
    half = [
        nt(onehot(iota((nc, NESTED * nc), 1) == NESTED * iota((nc, NESTED * nc), 0) + k), padded) for k in range(NESTED)
    ]
    bpt_ref[...] = jnp.where(iota((nc, pdev), 1) < 16, half[0], half[1])

    def second(dest, j):
        pltpu.make_async_remote_copy(
            src_ref=main_s2.at[dest],
            dst_ref=main_r2.at[me],
            send_sem=s2_sem,
            recv_sem=r2_sem.at[j],
            device_id={"comp": dest},
            device_id_type=pl.DeviceIdType.MESH,
        ).start()

    def give(j):
        for dy in range(yd):
            cols = pl.ds(dy * 2 * pdev, 2 * pdev)
            values = pick(col_ref[j, :, cols], row_ref[j, :, cols], 2 * pdev)
            for c in range(2):
                dest = 2 * chip_of(j, dy) + c
                mine = values[:, c * pdev : (c + 1) * pdev]
                listed_row = bpt_ref[pl.ds(dest, 1), :]
                for k in range(5):
                    two = mine[2 * k : 2 * k + 2] if k < 4 else jnp.concatenate([mine[8:], listed_row], axis=0)
                    main_s2[dest, k] = two.astype(BF16)

    def give_group(t, _):
        j = far_first(t)
        give(j)
        for dy in range(yd):
            for c in range(2):
                second(2 * chip_of(j, dy) + c, mirror(j))
        return 0

    lax.fori_loop(0, zd - 1, give_group, 0)
    give(zd - 1)
    for dy in range(1, yd):
        for c in range(2):
            second(2 * chip_of(zd - 1, dy) + c, zd - 1)
    second(me + 1 - 2 * my_core, zd - 1)
    main_r2[me] = main_s2[me]

    own = pl.ds(pl.multiple_of(my_core * pdev, pdev), pdev)
    at_slots = nn(sea.astype(BF16), col_ref[zd - 1, :, own]) * row_ref[zd - 1, :, own].astype(F32)
    live = jnp.sum(at_slots, axis=0, keepdims=True)

    kern_copy.wait()
    blocks = ncomp // pdev

    def turn(i, _):
        for k in range(blocks):
            tile = kern_ref[pl.ds(pl.multiple_of(i * pdev, pdev), pdev), k * pdev : (k + 1) * pdev]
            kernt_ref[k * pdev : (k + 1) * pdev, pl.ds(pl.multiple_of(i * pdev, pdev), pdev)] = (
                tile.T
            )
        return 0

    lax.fori_loop(0, blocks, turn, 0)

    def factors(i, _):
        rows = pl.ds(pl.multiple_of(i * pdev, pdev), pdev)
        gain = jnp.broadcast_to(gain_ref[pl.ds(i, 1), :], (pdev, pdev)).T
        grow_ref[rows, :] = 1.0 + gain * wind_ref[...]
        damp_b[rows, :] = jnp.broadcast_to(damp_ref[pl.ds(i, 1), :], (pdev, pdev)).T
        return 0

    lax.fori_loop(0, blocks, factors, 0)

    def gather(j, total):
        for dy in range(yd):
            chip = chip_of(j, dy)
            upper, lower = (
                jnp.concatenate([main_r2[2 * chip + c, k].astype(F32) for k in range(4)], axis=0) for c in range(2)
            )
            total = total + (upper + lower)
            prop_ref[pl.ds(pl.multiple_of(16 * chip, 16), 16), :] = jnp.concatenate([upper, lower], axis=0).astype(BF16)
            for c in range(2):
                pair = main_r2[2 * chip + c, 4].astype(F32)
                lastp_ref[pl.ds(2 * chip + c, 1), :] = pair[:1]
                listp_ref[pl.ds(2 * chip + c, 1), :] = pair[1:]
        return total

    def collect(t, total):
        j = far_first(t)
        arrived(r2_sem.at[j], main_r2, 2 * yd)
        return gather(j, total)

    total = lax.fori_loop(0, zd - 1, collect, jnp.zeros((8, pdev), F32))
    arrived(r2_sem.at[zd - 1], main_r2, 2 * yd - 1)
    total = gather(zd - 1, total)
    prop_ref[whole:, :] = lastp_ref[...].astype(BF16)
    energy = (jnp.sum(total, axis=0, keepdims=True) + jnp.sum(lastp_ref[...], axis=0, keepdims=True)) / ncomp

    got = listp_ref[...].astype(BF16)
    wanted = iota((pdev, ncomp), 1)
    owner_row = jnp.where(wanted < whole, wanted // 8, wanted - whole)
    which = jnp.where(wanted < whole, wanted % 8, 8)
    for k in range(NESTED):
        spread = nn(got, onehot(iota((pdev, ncomp), 0) == 16 * k + which))
        keep = iota((nc, ncomp), 0) == owner_row[:nc]
        bnd_ref[k : k + 1, :] = jnp.sum(jnp.where(keep, spread, 0.0), axis=0, keepdims=True).astype(BF16)

    big = 3 * pdev if blocks % 3 == 0 else pdev

    def cross(i, _):
        rows = pl.ds(pl.multiple_of(i * big, big), big)
        forward = nn(kern_ref[rows, :], prop_ref[...])
        backward = nn(kernt_ref[rows, :], prop_ref[...])
        cross_ref[rows, :] = (forward * backward).astype(BF16)
        return 0

    lax.fori_loop(0, ncomp // big, cross, 0)

    def finish(i, _):
        rows = pl.ds(pl.multiple_of(i * big, big), big)
        coupling = nn(kern_ref[rows, :], cross_ref[...])
        growth = grow_ref[rows, :] - damp_b[rows, :] * energy
        value = jnp.maximum(prop_ref[rows, :].astype(F32) * growth + 0.1 * coupling, 0.0) * live
        upd_ref[rows, :] = value.astype(BF16)
        return 0

    lax.fori_loop(0, ncomp // big, finish, 0)

    arrived(s1_sem.at[0], main_r1, nc - 1)
    arrived(s1_sem.at[1], last_r1, nc - 1)
    arrived(s2_sem, main_r2, nc - 1)


def body(
    spectra,
    kernel,
    wind_gain,
    damping,
    wind_speed,
    class_speed,
    depth_class,
    cell_of_point,
    sea_mask,
    bnd_owner,
    bnd_slot,
):
    ncomp, pdev = spectra.shape
    nc = lax.axis_size("comp")
    nnest = lax.axis_size("nest")
    srows, gy = sea_mask.shape
    nclass = class_speed.shape[0]
    blocks = ncomp // pdev
    angles = np.arange(NDIR, dtype=np.float32) * np.float32(2.0 * math.pi / NDIR)
    comp_dir = np.arange(ncomp) % NDIR
    cosines = jnp.asarray(np.cos(angles)[comp_dir], F32)
    sines = jnp.asarray(np.sin(angles)[comp_dir], F32)
    vmem = pl.BlockSpec(memory_space=pltpu.VMEM)
    sizes = (nc, ncomp, pdev, srows, gy, nclass, nnest)
    span = YDIM * 2 * pdev
    updated, boundary = pl.pallas_call(
        functools.partial(step_kernel, sizes),
        out_shape=(
            jax.ShapeDtypeStruct((ncomp, pdev), BF16),
            jax.ShapeDtypeStruct((NESTED, ncomp), BF16),
        ),
        in_specs=[pl.BlockSpec(memory_space=pl.ANY)] * 13,
        out_specs=(vmem, vmem),
        scratch_shapes=[
            pltpu.VMEM((ncomp // 8, 8, pdev), BF16),
            pltpu.VMEM((blocks, pdev), F32),
            pltpu.VMEM((blocks, pdev), F32),
            pltpu.VMEM((1, pdev), F32),
            pltpu.SMEM(class_speed.shape, F32),
            pltpu.SMEM((ncomp,), F32),
            pltpu.SMEM((ncomp,), F32),
            pltpu.VMEM((nc, pdev), I32),
            pltpu.VMEM((nc, pdev), I32),
            pltpu.VMEM((srows, gy), I32),
            pltpu.VMEM((1, NESTED * nc), I32),
            pltpu.VMEM((1, NESTED * nc), I32),
            pltpu.VMEM((nc, pdev), F32),
            pltpu.VMEM((nc, pdev), F32),
            pltpu.VMEM((nc, pdev), F32),
            pltpu.VMEM((ZDIM, gy, span), BF16),
            pltpu.VMEM((ZDIM, srows, span), BF16),
            pltpu.VMEM((gy, NESTED * nc), BF16),
            pltpu.VMEM((srows, NESTED * nc), BF16),
            pltpu.VMEM((9 * srows, span), BF16),
            pltpu.VMEM((9 * srows, gy), F32),
            pltpu.VMEM((3, srows, gy), F32),
            pltpu.VMEM((9, srows, gy), F32),
            pltpu.VMEM((9 * srows, gy), BF16),
            pltpu.VMEM((nc, 1, pdev), F32),
            pltpu.VMEM((nc, 8, pdev), BF16),
            pltpu.VMEM((nc, 1, pdev), F32),
            pltpu.VMEM((nc, 5, 2, pdev), BF16),
            pltpu.VMEM((nc, 5, 2, pdev), BF16),
            pltpu.VMEM((nc, pdev), F32),
            pltpu.VMEM((nc, pdev), F32),
            pltpu.VMEM((nc, pdev), F32),
            pltpu.VMEM((2, 16, gy), F32),
            pltpu.VMEM((2, 16, gy), F32),
            pltpu.VMEM((ncomp, pdev), BF16),
            pltpu.VMEM((ncomp, ncomp), BF16),
            pltpu.VMEM((ncomp, ncomp), BF16),
            pltpu.VMEM((ncomp, pdev), F32),
            pltpu.VMEM((ncomp, pdev), F32),
            pltpu.VMEM((ncomp, pdev), BF16),
            pltpu.SemaphoreType.DMA,
            pltpu.SemaphoreType.DMA((12,)),
            pltpu.SemaphoreType.DMA((2,)),
            pltpu.SemaphoreType.DMA((2, ZDIM)),
            pltpu.SemaphoreType.DMA,
            pltpu.SemaphoreType.DMA((ZDIM,)),
            pltpu.SemaphoreType.DMA((2, 2)),
        ],
        compiler_params=pltpu.CompilerParams(collective_id=0, has_side_effects=True),
    )(
        kernel,
        spectra.reshape(ncomp // 8, 8, pdev),
        wind_gain.reshape(blocks, pdev),
        damping.reshape(blocks, pdev),
        wind_speed.reshape(1, pdev),
        class_speed,
        cosines,
        sines,
        depth_class.reshape(nc, pdev),
        cell_of_point.reshape(nc, pdev),
        sea_mask,
        bnd_owner,
        bnd_slot,
    )
    return updated, boundary[None]


def solution(mesh):
    placed = (
        P(None, ("nest", "comp")),
        P(),
        P(),
        P(),
        P(("nest", "comp")),
        P(),
        P("nest", None),
        P("nest", None),
        P("nest", None),
        P("nest", None),
        P("nest", None),
    )
    return jax.shard_map(
        body,
        mesh=mesh,
        in_specs=placed,
        out_specs=(P(None, ("nest", "comp")), P("nest", "comp", None)),
        check_vma=False,
    )
```
